32 devices in a mesh: grp: 4 (over x, core), slab: 8 (over z, y).
Axes of the slice: x: 2, y: 2, z: 4, core: 2. Of those that a mesh axis runs over, the one named last changes fastest.
Arguments:
- fine_noise: float32 [8, 4, 4, 256, 512], P('slab', 'grp'), may hold values from -6 to 6
- fine_kappa: float32 [8, 4, 4, 256, 512], P('slab', 'grp'), may hold values from 0.05 to 4
- coarse_kappa: float32 [64, 128, 256], P('slab', 'grp'), may hold values from 0.05 to 4
Outputs:
- fine_stiffness: float32 [8, 4, 4, 256, 512], P('slab', 'grp')
- coarse_stiffness: float32 [64, 128, 256], P('slab', 'grp')
The draws below stay inside these ranges and needn't reach their ends.
All inputs are finite; a program needn't handle non-finite values.
Results may differ from the reference program's by a relative error of at most 0.00002.
Values sent between devices are 32-bit elements; how exact they have to be, the bound alone decides.
No kernel may reach another device: no remote copies, remote signals or barrier semaphores. Data moves between devices by JAX's collectives and lax.ppermute only.
A program may use at most 320 MiB of HBM per device.

```python
import math
import jax
import jax.numpy as jnp

FX = 256
FY = 512
FZD = 4
SWEEPS = 4
FZ = 128
CZ = 64
N_GRP = 4
N_SLAB = 8


def steps_of(rng, extent, shards, low, largest):
    factor_of, own = 1.0, jax.random.fold_in(rng, 6)
    for position, shards_of in shards:
        heights = jnp.exp(jax.random.uniform(jax.random.fold_in(own, position), (shards_of,), jnp.float32, low / len(shards), largest / len(shards)))
        factor_of = factor_of * jnp.repeat(heights, extent[position] // shards_of).reshape([-1 if axis == position else 1 for axis in range(len(extent))])
    return factor_of


def bell_draw(rng, shape, spread, most, split=(), held_as=jnp.bfloat16):
    entries = spread * jax.random.normal(rng, shape, jnp.float32)
    if split:
        entries = entries * steps_of(rng, shape, split, -0.22, 0.18)
    return jnp.clip(entries, -most, most).astype(held_as)


def setup_inputs(seed: int = 0) -> dict:
    splits = jax.random.split(jax.random.key(seed), 4)
    fine_noise = bell_draw(splits[0], (N_SLAB, N_GRP, FZD, FX, FY), 1.0, 6.0, ((0, 8), (1, 4)), jnp.float32)
    fine_kappa = jnp.clip(jnp.exp(math.log(4.0) - 4.3820266 * jax.random.uniform(splits[1], (N_SLAB, N_GRP, FZD, FX, FY), jnp.float32) ** steps_of(splits[1], (N_SLAB, N_GRP, FZD, FX, FY), ((0, 8), (1, 4)), -0.2, 0.2)), 0.05, 4.0)
    coarse_kappa = jnp.clip(jnp.exp(math.log(4.0) - 4.3820266 * jax.random.uniform(splits[2], (CZ, FX // 2, FY // 2), jnp.float32) ** steps_of(splits[2], (CZ, FX // 2, FY // 2), ((0, 8), (1, 4)), -0.2, 0.2)), 0.05, 4.0)
    return dict(fine_noise=fine_noise, fine_kappa=fine_kappa, coarse_kappa=coarse_kappa)


def neighbours(field):
    padded = jnp.pad(field, 1)
    total = padded[2:, 1:-1, 1:-1] + padded[:-2, 1:-1, 1:-1]
    total = total + padded[1:-1, 2:, 1:-1] + padded[1:-1, :-2, 1:-1]
    total = total + padded[1:-1, 1:-1, 2:] + padded[1:-1, 1:-1, :-2]
    return total


def reference(fine_noise, fine_kappa, coarse_kappa):
    noise_grid = fine_noise.reshape(FZ, FX, FY)
    kappa_grid = fine_kappa.reshape(FZ, FX, FY)
    coarse_noise = 0.125 * noise_grid.reshape(FZ // 2, 2, FX // 2, 2, FY // 2, 2).sum(axis=(1, 3, 5))
    fine_diag = 6.0 + kappa_grid
    fine_field = jnp.zeros_like(noise_grid)
    for step in range(SWEEPS):
        fine_field = (noise_grid + neighbours(fine_field)) / fine_diag
    coarse_diag = 1.5 + coarse_kappa
    coarse_field = jnp.zeros_like(coarse_noise)
    for step in range(SWEEPS):
        coarse_field = (coarse_noise + 0.25 * neighbours(coarse_field)) / coarse_diag
    fine_stiffness = jnp.exp(fine_field).reshape(fine_noise.shape)
    return fine_stiffness, jnp.exp(coarse_field)
```

```python
import functools

import jax
import jax.numpy as jnp
from jax import lax
from jax.experimental import pallas as pl
from jax.experimental.pallas import tpu as pltpu
from jax.sharding import PartitionSpec as P

SWEEPS = 4
HALO = SWEEPS - 1
ROWPAD = 4
STRIP = 32
LIMIT = 56 * 1024 * 1024


def whole():
    return pl.BlockSpec(memory_space=pltpu.VMEM)


def scalar():
    return pl.BlockSpec(memory_space=pltpu.SMEM)


def anywhere():
    return pl.BlockSpec(memory_space=pl.ANY)


def cost(cells, ops, arrays, transcendentals=0):
    return pl.CostEstimate(
        flops=cells * ops, bytes_accessed=4 * cells * arrays, transcendentals=transcendentals
    )


def lane_sum(c):
    cols = c.shape[-1]
    lane = lax.broadcasted_iota(jnp.int32, c.shape, c.ndim - 1)
    left = jnp.where(lane == 0, 0.0, pltpu.roll(c, 1, axis=c.ndim - 1))
    right = jnp.where(lane == cols - 1, 0.0, pltpu.roll(c, cols - 1, axis=c.ndim - 1))
    return left + right


def plane_sum(load, start, size, rows):
    c = load(start, size)
    above = load(pl.multiple_of(jnp.maximum(start - 8, 0), 8), 8)[7:8]
    below = load(pl.multiple_of(jnp.minimum(start + size, rows - 8), 8), 8)[0:1]
    above = jnp.where(start > 0, above, 0.0)
    below = jnp.where(start + size < rows, below, 0.0)
    sub = lax.broadcasted_iota(jnp.int32, c.shape, 0)
    up = jnp.where(sub == 0, above, pltpu.roll(c, 1, axis=0))
    down = jnp.where(sub == size - 1, below, pltpu.roll(c, size - 1, axis=0))
    return (up + down) + lane_sum(c)


def loader(ref, *lead):
    return lambda start, size: ref[(*lead, pl.ds(start, size), slice(None))]


def strips(rows, body):
    @pl.loop(0, rows // STRIP)
    def _(k):
        body(pl.multiple_of(k * STRIP, STRIP))


def advance(field, b, r, rows, face_off, face_on, mid):
    depth = len(field)

    def body(i):
        for m in range(depth):
            total = plane_sum(field[m], i, STRIP, rows)
            if m > 0:
                total = total + field[m - 1](i, STRIP)
            if m < depth - 1:
                total = total + field[m + 1](i, STRIP)
            rows_of = pl.ds(i, STRIP)
            value = b[m, rows_of, :] + r[m, rows_of, :] * total
            if m == 0:
                face_off[rows_of, :] = value
            elif m == depth - 1:
                face_on[rows_of, :] = value
            else:
                mid(m - 1, rows_of, value)

    strips(rows, body)


def first_kernel(flip_ref, noise, kappa, b, r, part_off, part_on, mid):
    depth, rows, _ = b.shape
    flip = flip_ref[0]

    def prepare(i):
        for m in range(depth):
            src = m + flip * (depth - 1 - 2 * m)
            at = pl.ds(i, STRIP)
            inverse = 1.0 / (6.0 + kappa[src, at, :])
            r[m, at, :] = inverse
            b[m, at, :] = noise[src, at, :] * inverse

    strips(rows, prepare)
    field = [loader(b, m) for m in range(depth)]

    def put(m, at, value):
        mid[m, at, :] = value

    advance(field, b, r, rows, part_off, part_on, put)


def middle_kernel(off, on, old_mid, b, r, part_off, part_on, mid):
    depth, rows, _ = b.shape
    field = [loader(off)] + [loader(old_mid, m) for m in range(depth - 2)] + [loader(on)]

    def put(m, at, value):
        mid[m, at, :] = value

    advance(field, b, r, rows, part_off, part_on, put)


def last_kernel(flip_ref, off, on, old_mid, b, r, part_off, part_on, out, mid, sems):
    depth, rows, _ = b.shape
    flip = flip_ref[0]
    field = [loader(off)] + [loader(old_mid, m) for m in range(depth - 2)] + [loader(on)]

    def put(m, at, value):
        mid[m, at, :] = jnp.exp(value)

    advance(field, b, r, rows, part_off, part_on, put)
    copies = []
    for m in range(1, depth - 1):
        dst = m + flip * (depth - 1 - 2 * m)
        copies.append(pltpu.make_async_copy(mid.at[m - 1], out.at[dst], sems.at[m - 1]))
    for copy in copies:
        copy.start()
    for copy in copies:
        copy.wait()


def face_kernel(layer_ref, part, r, halo, old, out):
    del layer_ref, old
    out[0] = jnp.exp(part[...] + r[0] * halo[...])


def restrict_kernel(place_ref, noise, kappa, blocks, pair, fine_rows):
    depth, rows, cols = noise.shape
    groups = blocks.shape[0]
    half_rows, half_cols = rows // 2, cols // 2
    own_rows = half_rows // groups
    span = own_rows + 2 * ROWPAD
    position = place_ref[0]
    src = lax.broadcasted_iota(jnp.int32, (cols, half_cols), 0)
    dst = lax.broadcasted_iota(jnp.int32, (cols, half_cols), 1)
    fold = jnp.where(src // 2 == dst, 0.125, 0.0).astype(jnp.bfloat16)
    zero = jnp.zeros((8, half_cols), jnp.float32)
    for layer in range(depth // 2):
        pair[...] = noise[2 * layer] + noise[2 * layer + 1]
        cut = cols // 128
        pieces = []
        for c in range(cut):
            fine_rows[...] = pair[:, 128 * c : 128 * (c + 1)]
            pieces.append(
                fine_rows[pl.ds(0, half_rows, stride=2), :]
                + fine_rows[pl.ds(1, half_rows, stride=2), :]
            )
        summed = jnp.concatenate(pieces, axis=1)
        high = summed.astype(jnp.bfloat16)
        rest = summed - high.astype(jnp.float32)
        middle = rest.astype(jnp.bfloat16)
        low = (rest - middle.astype(jnp.float32)).astype(jnp.bfloat16)
        dot = functools.partial(jnp.dot, preferred_element_type=jnp.float32)
        coarse = dot(low, fold) + dot(middle, fold) + dot(high, fold)
        padded = jnp.concatenate([zero[:ROWPAD], coarse, zero[:ROWPAD]], axis=0)
        for g in range(groups):
            blocks[g, layer * span : (layer + 1) * span, :] = padded[
                g * own_rows : g * own_rows + span
            ]
    base = (depth // 2) * span
    layers = kappa.shape[0]
    for layer in range(layers):
        first = 1.0 / (1.5 + kappa[layer, 0:ROWPAD, :])
        last = 1.0 / (1.5 + kappa[layer, own_rows - ROWPAD : own_rows, :])
        for g in range(groups):
            sent = jnp.where(position + 1 == g, last, jnp.where(position - 1 == g, first, 0.0))
            blocks[g, base + layer * ROWPAD : base + (layer + 1) * ROWPAD, :] = sent


def frame_kernel(place_ref, blocks, kappa, own, up, down):
    groups = blocks.shape[0]
    layers, own_rows, _ = kappa.shape
    span = own_rows + 2 * ROWPAD
    per = layers // groups
    base = per * span
    position = place_ref[0]
    for layer in range(layers):
        g, k = layer // per, layer % per
        noise = blocks[g, k * span : (k + 1) * span, :]
        at = slice(base + layer * ROWPAD, base + (layer + 1) * ROWPAD)
        top = jnp.where(position > 0, blocks[jnp.maximum(position - 1, 0), at, :], 0.0)
        bottom = jnp.where(
            position < groups - 1, blocks[jnp.minimum(position + 1, groups - 1), at, :], 0.0
        )
        middle = 1.0 / (1.5 + kappa[layer])
        inverse = jnp.concatenate([top, middle, bottom], axis=0)
        own[0, layer] = noise
        own[1, layer] = inverse
        if layer < HALO:
            down[0, layer] = noise
            down[1, layer] = inverse
        if layer >= layers - HALO:
            up[0, layer - layers + HALO] = noise
            up[1, layer - layers + HALO] = inverse


def coarse_kernel(own, below, above, out, b, r, even, odd):
    layers, own_rows, _ = out.shape
    total_layers, span, cols = b.shape
    total = total_layers

    def prepare(dst, ref, src):
        inverse = ref[1, src]
        r[dst] = 0.25 * inverse
        b[dst] = ref[0, src] * inverse

    for k in range(HALO):
        prepare(k, below, k)
        prepare(HALO + layers + k, above, k)

    @pl.loop(0, layers)
    def _(k):
        prepare(HALO + k, own, k)

    sub = lax.broadcasted_iota(jnp.int32, (span, cols), 0)

    def sweep(src, layer):
        c = src[layer]
        up = jnp.where(sub == 0, 0.0, pltpu.roll(c, 1, axis=0))
        dn = jnp.where(sub == span - 1, 0.0, pltpu.roll(c, span - 1, axis=0))
        near = (up + dn) + lane_sum(c) + (src[layer - 1] + src[layer + 1])
        return b[layer] + r[layer] * near

    source = b
    for step in range(1, SWEEPS):
        target = odd if step % 2 else even
        if step < SWEEPS - 1:

            @pl.loop(step, total - step)
            def _(layer):
                target[layer] = sweep(source, layer)

        else:

            @pl.loop(HALO, HALO + layers)
            def _(layer):
                value = jnp.exp(sweep(source, layer))
                out[layer - HALO] = value[ROWPAD : ROWPAD + own_rows]

        source = target


def body(axes, fine_noise, fine_kappa, coarse_kappa):
    noise = fine_noise[0, 0]
    kappa = fine_kappa[0, 0]
    depth, rows, cols = noise.shape
    layers, own_rows, half_cols = coarse_kappa.shape
    groups, slabs = lax.axis_size("grp"), lax.axis_size("slab")
    count = groups * slabs
    size = {"grp": groups, "slab": slabs}

    def flat(link):
        where = {"grp": link % groups, "slab": link // groups}
        index = 0
        for axis in axes:
            index = index * size[axis] + where[axis]
        return index

    near, far = [], []
    for link in range(count - 1):
        both = [(flat(link), flat(link + 1)), (flat(link + 1), flat(link))]
        (far if link % 2 else near).extend(both)
    position = lax.axis_index("grp")
    flip = (position % 2).astype(jnp.int32)
    flip1 = flip[None]
    place = position.astype(jnp.int32)[None]
    params = pltpu.CompilerParams(vmem_limit_bytes=LIMIT)
    cells = rows * cols
    plane = jax.ShapeDtypeStruct((rows, cols), jnp.float32)
    stack = jax.ShapeDtypeStruct((depth, rows, cols), jnp.float32)
    inner = jax.ShapeDtypeStruct((depth - 2, rows, cols), jnp.float32)

    def swap(off, on):
        return lax.ppermute(off, axes, far), lax.ppermute(on, axes, near)

    def face(layer):
        n = lax.dynamic_index_in_dim(noise, layer, 0, keepdims=False)
        k = lax.dynamic_index_in_dim(kappa, layer, 0, keepdims=False)
        return n / (6.0 + k)

    index_off = flip * (depth - 1)
    index_on = (1 - flip) * (depth - 1)
    halo_off, halo_on = swap(face(index_off), face(index_on))

    span = own_rows + 2 * ROWPAD
    block_rows = (depth // 2) * span + layers * ROWPAD
    blocks = pl.pallas_call(
        restrict_kernel,
        name="restrict",
        out_shape=jax.ShapeDtypeStruct((groups, block_rows, half_cols), jnp.float32),
        in_specs=[scalar(), whole(), whole()],
        out_specs=whole(),
        scratch_shapes=[
            pltpu.VMEM((rows, cols), jnp.float32),
            pltpu.VMEM((rows, 128), jnp.float32),
        ],
        compiler_params=params,
        cost_estimate=cost(cells * depth, 8, 1),
    )(place, noise, coarse_kappa)
    blocks = lax.all_to_all(blocks, "grp", split_axis=0, concat_axis=0, tiled=True)

    b, r, part_off, part_on, mid = pl.pallas_call(
        first_kernel,
        name="first",
        out_shape=(stack, stack, plane, plane, inner),
        in_specs=[scalar(), whole(), whole()],
        out_specs=(whole(),) * 5,
        compiler_params=params,
        cost_estimate=cost(cells * depth, 16, 5),
    )(flip1, noise, kappa)

    edge = jax.ShapeDtypeStruct((2, HALO, span, half_cols), jnp.float32)
    own, up, down = pl.pallas_call(
        frame_kernel,
        name="frame",
        out_shape=(
            jax.ShapeDtypeStruct((2, layers, span, half_cols), jnp.float32),
            edge,
            edge,
        ),
        in_specs=[scalar(), whole(), whole()],
        out_specs=(whole(),) * 3,
        compiler_params=params,
        cost_estimate=cost(layers * span * half_cols, 4, 5),
    )(place, blocks, coarse_kappa)
    ahead = [(i, i + 1) for i in range(slabs - 1)]
    back = [(i + 1, i) for i in range(slabs - 1)]
    below = lax.ppermute(up, "slab", ahead)
    above = lax.ppermute(down, "slab", back)

    off = part_off + r[0] * halo_off
    on = part_on + r[depth - 1] * halo_on
    halo_off, halo_on = swap(off, on)
    part_off, part_on, mid = pl.pallas_call(
        middle_kernel,
        name="middle",
        out_shape=(plane, plane, inner),
        in_specs=[whole()] * 5,
        out_specs=(whole(),) * 3,
        compiler_params=params,
        cost_estimate=cost(cells * depth, 12, 4),
    )(off, on, mid, b, r)

    off = part_off + r[0] * halo_off
    on = part_on + r[depth - 1] * halo_on
    halo_off, halo_on = swap(off, on)
    part_off, part_on, fine = pl.pallas_call(
        last_kernel,
        name="last",
        out_shape=(plane, plane, stack),
        in_specs=[scalar()] + [whole()] * 5,
        out_specs=(whole(), whole(), anywhere()),
        scratch_shapes=[
            pltpu.VMEM((depth - 2, rows, cols), jnp.float32),
            pltpu.SemaphoreType.DMA((depth - 2,)),
        ],
        compiler_params=params,
        cost_estimate=cost(cells * depth, 14, 4, cells * 2),
    )(flip1, off, on, mid, b, r)

    framed = (layers + 2 * HALO, span, half_cols)
    coarse = pl.pallas_call(
        coarse_kernel,
        name="coarse",
        out_shape=jax.ShapeDtypeStruct(coarse_kappa.shape, jnp.float32),
        in_specs=[whole()] * 3,
        out_specs=whole(),
        scratch_shapes=[pltpu.VMEM(framed, jnp.float32)] * 4,
        compiler_params=params,
        cost_estimate=cost(layers * own_rows * half_cols, 80, 6),
    )(own, below, above)

    tile = rows // 4

    def finish(fine, layer, source, part, halo):
        return pl.pallas_call(
            face_kernel,
            name="face",
            out_shape=stack,
            grid_spec=pltpu.PrefetchScalarGridSpec(
                num_scalar_prefetch=1,
                grid=(rows // tile,),
                in_specs=[
                    pl.BlockSpec((tile, cols), lambda i, at: (i, 0)),
                    pl.BlockSpec((1, tile, cols), lambda i, at: (source, i, 0)),
                    pl.BlockSpec((tile, cols), lambda i, at: (i, 0)),
                    anywhere(),
                ],
                out_specs=pl.BlockSpec((1, tile, cols), lambda i, at: (at[0], i, 0)),
            ),
            input_output_aliases={4: 0},
            compiler_params=params,
            cost_estimate=cost(cells, 3, 4, cells),
        )(layer[None], part, r, halo, fine)

    fine = finish(fine, index_on, depth - 1, part_on, halo_on)
    fine = finish(fine, index_off, 0, part_off, halo_off)
    return fine[None, None], coarse


def solution(mesh):
    return jax.shard_map(
        functools.partial(body, tuple(mesh.axis_names)),
        mesh=mesh,
        in_specs=(
            P("slab", "grp", None, None, None),
            P("slab", "grp", None, None, None),
            P("slab", "grp", None),
        ),
        out_specs=(P("slab", "grp", None, None, None), P("slab", "grp", None)),
        check_vma=False,
    )
```

```python
import functools

import jax
import jax.numpy as jnp
from jax import lax
from jax.experimental import pallas as pl
from jax.experimental.pallas import tpu as pltpu
from jax.sharding import PartitionSpec as P

SWEEPS = 4
HALO = SWEEPS - 1
ROWPAD = 4
STRIP = 32
FACE_TILES = 4
LIMIT = 12 * 1024 * 1024


def whole():
    return pl.BlockSpec(memory_space=pltpu.VMEM)


def scalar():
    return pl.BlockSpec(memory_space=pltpu.SMEM)


def anywhere():
    return pl.BlockSpec(memory_space=pl.ANY)


def cost(cells, ops, arrays, transcendentals=0):
    return pl.CostEstimate(
        flops=cells * ops, bytes_accessed=4 * cells * arrays, transcendentals=transcendentals
    )


def lane_sum(c):
    cols = c.shape[-1]
    lane = lax.broadcasted_iota(jnp.int32, c.shape, c.ndim - 1)
    left = jnp.where(lane == 0, 0.0, pltpu.roll(c, 1, axis=c.ndim - 1))
    right = jnp.where(lane == cols - 1, 0.0, pltpu.roll(c, cols - 1, axis=c.ndim - 1))
    return left + right


def plane_sum(load, start, size, rows):
    c = load(start, size)
    above = load(pl.multiple_of(jnp.maximum(start - 8, 0), 8), 8)[7:8]
    below = load(pl.multiple_of(jnp.minimum(start + size, rows - 8), 8), 8)[0:1]
    above = jnp.where(start > 0, above, 0.0)
    below = jnp.where(start + size < rows, below, 0.0)
    sub = lax.broadcasted_iota(jnp.int32, c.shape, 0)
    up = jnp.where(sub == 0, above, pltpu.roll(c, 1, axis=0))
    down = jnp.where(sub == size - 1, below, pltpu.roll(c, size - 1, axis=0))
    return (up + down) + lane_sum(c)


def loader(ref, *lead):
    return lambda start, size: ref[(*lead, pl.ds(start, size), slice(None))]


def strips(rows, body):
    @pl.loop(0, rows // STRIP)
    def _(k):
        body(pl.multiple_of(k * STRIP, STRIP))


def advance(field, b, r, rows, face_off, face_on, mid):
    depth = len(field)

    def body(i):
        for m in range(depth):
            total = plane_sum(field[m], i, STRIP, rows)
            if m > 0:
                total = total + field[m - 1](i, STRIP)
            if m < depth - 1:
                total = total + field[m + 1](i, STRIP)
            rows_of = pl.ds(i, STRIP)
            value = b[m, rows_of, :] + r[m, rows_of, :] * total
            if m == 0:
                face_off[rows_of, :] = value
            elif m == depth - 1:
                face_on[rows_of, :] = value
            else:
                mid(m - 1, rows_of, value)

    strips(rows, body)


def first_kernel(flip_ref, noise, kappa, b, r, part_off, part_on, mid):
    depth, rows, _ = b.shape
    flip = flip_ref[0]

    def prepare(i):
        for m in range(depth):
            src = m + flip * (depth - 1 - 2 * m)
            at = pl.ds(i, STRIP)
            inverse = 1.0 / (6.0 + kappa[src, at, :])
            r[m, at, :] = inverse
            b[m, at, :] = noise[src, at, :] * inverse

    strips(rows, prepare)
    field = [loader(b, m) for m in range(depth)]

    def put(m, at, value):
        mid[m, at, :] = value

    advance(field, b, r, rows, part_off, part_on, put)


def middle_kernel(off, on, old_mid, b, r, part_off, part_on, mid):
    depth, rows, _ = b.shape
    field = [loader(off)] + [loader(old_mid, m) for m in range(depth - 2)] + [loader(on)]

    def put(m, at, value):
        mid[m, at, :] = value

    advance(field, b, r, rows, part_off, part_on, put)


def last_kernel(flip_ref, off, on, old_mid, b, r, part_off, part_on, out, mid, sems):
    depth, rows, _ = b.shape
    flip = flip_ref[0]
    field = [loader(off)] + [loader(old_mid, m) for m in range(depth - 2)] + [loader(on)]

    def put(m, at, value):
        mid[m, at, :] = jnp.exp(value)

    advance(field, b, r, rows, part_off, part_on, put)
    copies = []
    for m in range(1, depth - 1):
        dst = m + flip * (depth - 1 - 2 * m)
        copies.append(pltpu.make_async_copy(mid.at[m - 1], out.at[dst], sems.at[m - 1]))
    for copy in copies:
        copy.start()
    for copy in copies:
        copy.wait()


def face_kernel(source, layer_ref, part, r, halo, old, out, done, sems):
    del old
    rows = part.shape[0]
    tile = rows // FACE_TILES
    copies = []
    for k in range(FACE_TILES):
        at = pl.ds(k * tile, tile)
        done[at, :] = jnp.exp(part[at, :] + r[source, at, :] * halo[at, :])
        copies.append(
            pltpu.make_async_copy(done.at[at], out.at[layer_ref[0], at], sems.at[k])
        )
        copies[-1].start()
    for copy in copies:
        copy.wait()


def restrict_kernel(place_ref, noise, kappa, blocks, pair, fine_rows):
    depth, rows, cols = noise.shape
    groups = blocks.shape[0]
    half_rows, half_cols = rows // 2, cols // 2
    own_rows = half_rows // groups
    span = own_rows + 2 * ROWPAD
    position = place_ref[0]
    src = lax.broadcasted_iota(jnp.int32, (cols, half_cols), 0)
    dst = lax.broadcasted_iota(jnp.int32, (cols, half_cols), 1)
    fold = jnp.where(src // 2 == dst, 0.125, 0.0).astype(jnp.bfloat16)
    zero = jnp.zeros((8, half_cols), jnp.float32)
    for layer in range(depth // 2):
        pair[...] = noise[2 * layer] + noise[2 * layer + 1]
        cut = cols // 128
        pieces = []
        for c in range(cut):
            fine_rows[...] = pair[:, 128 * c : 128 * (c + 1)]
            pieces.append(
                fine_rows[pl.ds(0, half_rows, stride=2), :]
                + fine_rows[pl.ds(1, half_rows, stride=2), :]
            )
        summed = jnp.concatenate(pieces, axis=1)
        high = summed.astype(jnp.bfloat16)
        rest = summed - high.astype(jnp.float32)
        middle = rest.astype(jnp.bfloat16)
        low = (rest - middle.astype(jnp.float32)).astype(jnp.bfloat16)
        dot = functools.partial(jnp.dot, preferred_element_type=jnp.float32)
        coarse = dot(low, fold) + dot(middle, fold) + dot(high, fold)
        padded = jnp.concatenate([zero[:ROWPAD], coarse, zero[:ROWPAD]], axis=0)
        for g in range(groups):
            blocks[g, layer * span : (layer + 1) * span, :] = padded[
                g * own_rows : g * own_rows + span
            ]
    base = (depth // 2) * span
    layers = kappa.shape[0]
    for layer in range(layers):
        first = 1.0 / (1.5 + kappa[layer, 0:ROWPAD, :])
        last = 1.0 / (1.5 + kappa[layer, own_rows - ROWPAD : own_rows, :])
        for g in range(groups):
            sent = jnp.where(position + 1 == g, last, jnp.where(position - 1 == g, first, 0.0))
            blocks[g, base + layer * ROWPAD : base + (layer + 1) * ROWPAD, :] = sent


def frame_kernel(place_ref, blocks, kappa, own, up, down):
    groups = blocks.shape[0]
    layers, own_rows, _ = kappa.shape
    span = own_rows + 2 * ROWPAD
    per = layers // groups
    base = per * span
    position = place_ref[0]
    for layer in range(layers):
        g, k = layer // per, layer % per
        noise = blocks[g, k * span : (k + 1) * span, :]
        at = slice(base + layer * ROWPAD, base + (layer + 1) * ROWPAD)
        top = jnp.where(position > 0, blocks[jnp.maximum(position - 1, 0), at, :], 0.0)
        bottom = jnp.where(
            position < groups - 1, blocks[jnp.minimum(position + 1, groups - 1), at, :], 0.0
        )
        middle = 1.0 / (1.5 + kappa[layer])
        inverse = jnp.concatenate([top, middle, bottom], axis=0)
        own[0, layer] = noise
        own[1, layer] = inverse
        if layer < HALO:
            down[0, layer] = noise
            down[1, layer] = inverse
        if layer >= layers - HALO:
            up[0, layer - layers + HALO] = noise
            up[1, layer - layers + HALO] = inverse


def coarse_kernel(own, below, above, out, b, r, even, odd):
    layers, own_rows, _ = out.shape
    total_layers, span, cols = b.shape
    total = total_layers

    def prepare(dst, ref, src):
        inverse = ref[1, src]
        r[dst] = 0.25 * inverse
        b[dst] = ref[0, src] * inverse

    for k in range(HALO):
        prepare(k, below, k)
        prepare(HALO + layers + k, above, k)

    for k in range(layers):
        prepare(HALO + k, own, k)

    sub = lax.broadcasted_iota(jnp.int32, (span, cols), 0)

    def sweep(src, layer):
        c = src[layer]
        up = jnp.where(sub == 0, 0.0, pltpu.roll(c, 1, axis=0))
        dn = jnp.where(sub == span - 1, 0.0, pltpu.roll(c, span - 1, axis=0))
        near = (up + dn) + lane_sum(c) + (src[layer - 1] + src[layer + 1])
        return b[layer] + r[layer] * near

    source = b
    for step in range(1, SWEEPS):
        target = odd if step % 2 else even
        if step < SWEEPS - 1:

            for layer in range(step, total - step):
                target[layer] = sweep(source, layer)
        else:
            for layer in range(HALO, HALO + layers):
                value = jnp.exp(sweep(source, layer))
                out[layer - HALO] = value[ROWPAD : ROWPAD + own_rows]

        source = target


def body(axes, fine_noise, fine_kappa, coarse_kappa):
    noise = fine_noise[0, 0]
    kappa = fine_kappa[0, 0]
    depth, rows, cols = noise.shape
    layers, own_rows, half_cols = coarse_kappa.shape
    groups, slabs = lax.axis_size("grp"), lax.axis_size("slab")
    count = groups * slabs
    size = {"grp": groups, "slab": slabs}

    def flat(link):
        where = {"grp": link % groups, "slab": link // groups}
        index = 0
        for axis in axes:
            index = index * size[axis] + where[axis]
        return index

    near, far = [], []
    for link in range(count - 1):
        both = [(flat(link), flat(link + 1)), (flat(link + 1), flat(link))]
        (far if link % 2 else near).extend(both)
    position = lax.axis_index("grp")
    flip = (position % 2).astype(jnp.int32)
    flip1 = flip[None]
    place = position.astype(jnp.int32)[None]
    params = pltpu.CompilerParams(vmem_limit_bytes=LIMIT)
    cells = rows * cols
    plane = jax.ShapeDtypeStruct((rows, cols), jnp.float32)
    stack = jax.ShapeDtypeStruct((depth, rows, cols), jnp.float32)
    inner = jax.ShapeDtypeStruct((depth - 2, rows, cols), jnp.float32)

    def swap(off, on):
        return lax.ppermute(off, axes, far), lax.ppermute(on, axes, near)

    def face(layer):
        n = lax.dynamic_index_in_dim(noise, layer, 0, keepdims=False)
        k = lax.dynamic_index_in_dim(kappa, layer, 0, keepdims=False)
        return n / (6.0 + k)

    index_off = flip * (depth - 1)
    index_on = (1 - flip) * (depth - 1)
    first_off, index_on_later = lax.optimization_barrier((face(index_off), index_on))
    halo_off, halo_on = swap(first_off, face(index_on_later))

    span = own_rows + 2 * ROWPAD
    block_rows = (depth // 2) * span + layers * ROWPAD
    blocks = pl.pallas_call(
        restrict_kernel,
        name="restrict",
        out_shape=jax.ShapeDtypeStruct((groups, block_rows, half_cols), jnp.float32),
        in_specs=[scalar(), whole(), whole()],
        out_specs=whole(),
        scratch_shapes=[
            pltpu.VMEM((rows, cols), jnp.float32),
            pltpu.VMEM((rows, 128), jnp.float32),
        ],
        compiler_params=params,
        cost_estimate=cost(cells * depth, 8, 1),
    )(place, noise, coarse_kappa)
    blocks = lax.all_to_all(blocks, "grp", split_axis=0, concat_axis=0, tiled=True)

    b, r, part_off, part_on, mid = pl.pallas_call(
        first_kernel,
        name="first",
        out_shape=(stack, stack, plane, plane, inner),
        in_specs=[scalar(), whole(), whole()],
        out_specs=(whole(),) * 5,
        compiler_params=params,
        cost_estimate=cost(cells * depth, 16, 5),
    )(flip1, noise, kappa)

    off = part_off + r[0] * halo_off
    on = part_on + r[depth - 1] * halo_on
    off, on, blocks = lax.optimization_barrier((off, on, blocks))
    halo_off, halo_on = swap(off, on)
    edge = jax.ShapeDtypeStruct((2, HALO, span, half_cols), jnp.float32)
    own, up, down = pl.pallas_call(
        frame_kernel,
        name="frame",
        out_shape=(
            jax.ShapeDtypeStruct((2, layers, span, half_cols), jnp.float32),
            edge,
            edge,
        ),
        in_specs=[scalar(), whole(), whole()],
        out_specs=(whole(),) * 3,
        compiler_params=params,
        cost_estimate=cost(layers * span * half_cols, 4, 5),
    )(place, blocks, coarse_kappa)
    ahead = [(i, i + 1) for i in range(slabs - 1)]
    back = [(i + 1, i) for i in range(slabs - 1)]
    below = lax.ppermute(up, "slab", ahead)
    above = lax.ppermute(down, "slab", back)

    part_off, part_on, mid = pl.pallas_call(
        middle_kernel,
        name="middle",
        out_shape=(plane, plane, inner),
        in_specs=[whole()] * 5,
        out_specs=(whole(),) * 3,
        compiler_params=params,
        cost_estimate=cost(cells * depth, 12, 4),
    )(off, on, mid, b, r)

    off = part_off + r[0] * halo_off
    on = part_on + r[depth - 1] * halo_on
    off, on, below, above = lax.optimization_barrier((off, on, below, above))
    halo_off, halo_on = swap(off, on)
    part_off, part_on, fine = pl.pallas_call(
        last_kernel,
        name="last",
        out_shape=(plane, plane, stack),
        in_specs=[scalar()] + [whole()] * 5,
        out_specs=(whole(), whole(), anywhere()),
        scratch_shapes=[
            pltpu.VMEM((depth - 2, rows, cols), jnp.float32),
            pltpu.SemaphoreType.DMA((depth - 2,)),
        ],
        compiler_params=params,
        cost_estimate=cost(cells * depth, 14, 4, cells * 2),
    )(flip1, off, on, mid, b, r)

    framed = (layers + 2 * HALO, span, half_cols)
    coarse = pl.pallas_call(
        coarse_kernel,
        name="coarse",
        out_shape=jax.ShapeDtypeStruct(coarse_kappa.shape, jnp.float32),
        in_specs=[whole()] * 3,
        out_specs=whole(),
        scratch_shapes=[pltpu.VMEM(framed, jnp.float32)] * 4,
        compiler_params=params,
        cost_estimate=cost(layers * own_rows * half_cols, 80, 6),
    )(own, below, above)

    def finish(fine, layer, source, part, halo):
        return pl.pallas_call(
            functools.partial(face_kernel, source),
            name="face",
            out_shape=stack,
            in_specs=[scalar(), whole(), whole(), whole(), anywhere()],
            out_specs=anywhere(),
            scratch_shapes=[
                pltpu.VMEM((rows, cols), jnp.float32),
                pltpu.SemaphoreType.DMA((FACE_TILES,)),
            ],
            input_output_aliases={4: 0},
            compiler_params=params,
            cost_estimate=cost(cells, 3, 4, cells),
        )(layer[None], part, r, halo, fine)

    fine = finish(fine, index_on, depth - 1, part_on, halo_on)
    fine = finish(fine, index_off, 0, part_off, halo_off)
    return fine[None, None], coarse


def solution(mesh):
    return jax.shard_map(
        functools.partial(body, tuple(mesh.axis_names)),
        mesh=mesh,
        in_specs=(
            P("slab", "grp", None, None, None),
            P("slab", "grp", None, None, None),
            P("slab", "grp", None),
        ),
        out_specs=(P("slab", "grp", None, None, None), P("slab", "grp", None)),
        check_vma=False,
    )
```

```python
import functools

import jax
import jax.numpy as jnp
from jax import lax
from jax.experimental import pallas as pl
from jax.experimental.pallas import tpu as pltpu
from jax.sharding import PartitionSpec as P

SWEEPS = 4
HALO = SWEEPS - 1
ROWPAD = 4
STRIP = 32
FACE_TILES = 2
PIECES = 2
LIMIT = 12 * 1024 * 1024


def whole():
    return pl.BlockSpec(memory_space=pltpu.VMEM)


def scalar():
    return pl.BlockSpec(memory_space=pltpu.SMEM)


def anywhere():
    return pl.BlockSpec(memory_space=pl.ANY)


def cost(cells, ops, arrays, transcendentals=0):
    return pl.CostEstimate(flops=5000000000, bytes_accessed=1000000, transcendentals=0)
    return pl.CostEstimate(
        flops=cells * ops, bytes_accessed=4 * cells * arrays, transcendentals=transcendentals
    )


def lane_sum(c):
    cols = c.shape[-1]
    lane = lax.broadcasted_iota(jnp.int32, c.shape, c.ndim - 1)
    left = jnp.where(lane == 0, 0.0, pltpu.roll(c, 1, axis=c.ndim - 1))
    right = jnp.where(lane == cols - 1, 0.0, pltpu.roll(c, cols - 1, axis=c.ndim - 1))
    return left + right


def plane_sum(load, start, size, rows):
    c = load(start, size)
    above = load(pl.multiple_of(jnp.maximum(start - 8, 0), 8), 8)[7:8]
    below = load(pl.multiple_of(jnp.minimum(start + size, rows - 8), 8), 8)[0:1]
    above = jnp.where(start > 0, above, 0.0)
    below = jnp.where(start + size < rows, below, 0.0)
    sub = lax.broadcasted_iota(jnp.int32, c.shape, 0)
    up = jnp.where(sub == 0, above, pltpu.roll(c, 1, axis=0))
    down = jnp.where(sub == size - 1, below, pltpu.roll(c, size - 1, axis=0))
    return (up + down) + lane_sum(c)


def loader(ref, *lead):
    return lambda start, size: ref[(*lead, pl.ds(start, size), slice(None))]


def strips(rows, body):
    @pl.loop(0, rows // STRIP)
    def _(k):
        body(pl.multiple_of(k * STRIP, STRIP))


def advance(field, b, r, rows, face_off, face_on, mid):
    depth = len(field)

    def body(i):
        for m in range(depth):
            total = plane_sum(field[m], i, STRIP, rows)
            if m > 0:
                total = total + field[m - 1](i, STRIP)
            if m < depth - 1:
                total = total + field[m + 1](i, STRIP)
            rows_of = pl.ds(i, STRIP)
            value = b[m, rows_of, :] + r[m, rows_of, :] * total
            if m == 0:
                face_off[rows_of, :] = value
            elif m == depth - 1:
                face_on[rows_of, :] = value
            else:
                mid(m - 1, rows_of, value)

    strips(rows, body)


def first_kernel(flip_ref, noise, kappa, b, r, part_off, part_on, mid):
    depth, rows, _ = b.shape
    flip = flip_ref[0]

    def prepare(i):
        for m in range(depth):
            src = m + flip * (depth - 1 - 2 * m)
            at = pl.ds(i, STRIP)
            inverse = 1.0 / (6.0 + kappa[src, at, :])
            r[m, at, :] = inverse
            b[m, at, :] = noise[src, at, :] * inverse

    strips(rows, prepare)
    field = [loader(b, m) for m in range(depth)]

    def put(m, at, value):
        mid[m, at, :] = value

    advance(field, b, r, rows, part_off, part_on, put)


def meet_kernel(layer, start, part, halo, r, out):
    rows = out.shape[0]
    size = min(2 * STRIP, rows)
    for k in range(rows // size):
        at = pl.ds(k * size, size)
        of = pl.ds(start + k * size, size)
        out[at, :] = part[of, :] + r[layer, of, :] * halo[at, :]


def joined(pieces, whole_ref):
    rows = pieces[0].shape[0]
    for k, piece in enumerate(pieces):
        whole_ref[k * rows : (k + 1) * rows, :] = piece[...]


def middle_kernel(*refs):
    pieces = refs[:PIECES]
    on, old_mid, b, r, part_off, part_on, mid, off = refs[PIECES:]
    depth, rows, _ = b.shape
    joined(pieces, off)
    field = [loader(off)] + [loader(old_mid, m) for m in range(depth - 2)] + [loader(on)]

    def put(m, at, value):
        mid[m, at, :] = value

    advance(field, b, r, rows, part_off, part_on, put)


def last_kernel(flip_ref, *refs):
    pieces = refs[:PIECES]
    on, old_mid, b, r, part_off, part_on, out, mid, sems, off = refs[PIECES:]
    depth, rows, _ = b.shape
    joined(pieces, off)
    flip = flip_ref[0]
    field = [loader(off)] + [loader(old_mid, m) for m in range(depth - 2)] + [loader(on)]

    def put(m, at, value):
        mid[m, at, :] = jnp.exp(value)

    advance(field, b, r, rows, part_off, part_on, put)
    copies = []
    for m in range(1, depth - 1):
        dst = m + flip * (depth - 1 - 2 * m)
        copies.append(pltpu.make_async_copy(mid.at[m - 1], out.at[dst], sems.at[m - 1]))
    for copy in copies:
        copy.start()
    for copy in copies:
        copy.wait()


def face_kernel(source, start, layer_ref, part, r, halo, old, out, done, sems):
    del old
    tile = halo.shape[0] // FACE_TILES
    copies = []
    for k in range(FACE_TILES):
        at = pl.ds(k * tile, tile)
        of = pl.ds(start + k * tile, tile)
        done[at, :] = jnp.exp(part[of, :] + r[source, of, :] * halo[at, :])
        copies.append(
            pltpu.make_async_copy(done.at[at], out.at[layer_ref[0], of], sems.at[k])
        )
        copies[-1].start()
    for copy in copies:
        copy.wait()


def restrict_kernel(place_ref, noise, kappa, far, near, own, pair, fine_rows, padded):
    depth, rows, cols = noise.shape
    half_rows, half_cols = rows // 2, cols // 2
    own_rows = kappa.shape[1]
    span = own_rows + 2 * ROWPAD
    part = (depth // 2) * span
    position = place_ref[0]
    src = lax.broadcasted_iota(jnp.int32, (cols, half_cols), 0)
    dst = lax.broadcasted_iota(jnp.int32, (cols, half_cols), 1)
    fold = jnp.where(src // 2 == dst, 0.125, 0.0).astype(jnp.bfloat16)
    padded[...] = jnp.zeros_like(padded)
    flip1 = 1 - 2 * (position % 2)
    other = position + flip1
    across = jnp.where(position < 2, position + 2, position - 2)
    beyond = across + flip1
    for layer in range(depth // 2):
        pair[...] = noise[2 * layer] + noise[2 * layer + 1]
        pieces = []
        for c in range(cols // 128):
            fine_rows[...] = pair[:, 128 * c : 128 * (c + 1)]
            pieces.append(
                fine_rows[pl.ds(0, half_rows, stride=2), :]
                + fine_rows[pl.ds(1, half_rows, stride=2), :]
            )
        summed = jnp.concatenate(pieces, axis=1)
        high = summed.astype(jnp.bfloat16)
        rest = summed - high.astype(jnp.float32)
        middle = rest.astype(jnp.bfloat16)
        low = (rest - middle.astype(jnp.float32)).astype(jnp.bfloat16)
        dot = functools.partial(jnp.dot, preferred_element_type=jnp.float32)
        coarse = dot(low, fold) + dot(middle, fold) + dot(high, fold)
        padded[ROWPAD : ROWPAD + half_rows, :] = coarse
        at = slice(layer * span, (layer + 1) * span)

        def rows_of(g):
            return padded[pl.ds(pl.multiple_of(g * own_rows, 8), span), :]

        own[at, :] = rows_of(position)
        near[at, :] = rows_of(other)
        far[at, :] = rows_of(across)
        far[part + layer * span : part + (layer + 1) * span, :] = rows_of(beyond)
    for layer in range(kappa.shape[0]):
        first = 1.0 / (1.5 + kappa[layer, 0:ROWPAD, :])
        last = 1.0 / (1.5 + kappa[layer, own_rows - ROWPAD : own_rows, :])
        at = layer * ROWPAD
        far[2 * part + at : 2 * part + at + ROWPAD, :] = jnp.where(position < 2, last, first)
        near[part + at : part + at + ROWPAD, :] = jnp.where(position % 2 == 0, last, first)


def relay_kernel(near, arrived, out):
    mine = near.shape[0]
    carried = out.shape[0] - mine
    out[0:mine, :] = near[...]
    out[mine:, :] = arrived[arrived.shape[0] - carried :, :]


def frame_kernel(place_ref, kept, across, near, kappa, own, up, down):
    layers, own_rows, _ = kappa.shape
    span = own_rows + 2 * ROWPAD
    per = kept.shape[0] // span
    part = per * span
    edge = layers * ROWPAD
    position = place_ref[0]
    flip1 = 1 - 2 * (position % 2)
    beyond_chip = jnp.where(position < 2, position + 2, position - 2)
    for k in range(per):
        at = slice(k * span, (k + 1) * span)
        own[0, per * position + k] = kept[at, :]
        own[0, per * (position + flip1) + k] = near[at, :]
        own[0, per * beyond_chip + k] = across[at, :]
        relayed = slice(part + edge + k * span, part + edge + (k + 1) * span)
        own[0, per * (beyond_chip + flip1) + k] = near[relayed, :]
    for layer in range(layers):
        at = layer * ROWPAD
        direct = near[part + at : part + at + ROWPAD, :]
        passed = near[2 * part + edge + at : 2 * part + edge + at + ROWPAD, :]
        inner = jnp.logical_or(position == 1, position == 2)
        passed = jnp.where(inner, passed, 0.0)
        even = position % 2 == 0
        top = jnp.where(even, passed, direct)
        bottom = jnp.where(even, direct, passed)
        middle = 1.0 / (1.5 + kappa[layer])
        own[1, layer] = jnp.concatenate([top, middle, bottom], axis=0)
    for k in range(HALO):
        for half in range(2):
            down[half, k] = own[half, k]
            up[half, k] = own[half, layers - HALO + k]


def coarse_kernel(own, below, above, out, b, r, even, odd):
    layers, own_rows, _ = out.shape
    total_layers, span, cols = b.shape
    total = total_layers

    def prepare(dst, ref, src):
        inverse = ref[1, src]
        r[dst] = 0.25 * inverse
        b[dst] = ref[0, src] * inverse

    for k in range(HALO):
        prepare(k, below, k)
        prepare(HALO + layers + k, above, k)

    for k in range(layers):
        prepare(HALO + k, own, k)

    sub = lax.broadcasted_iota(jnp.int32, (span, cols), 0)

    def sweep(src, layer):
        c = src[layer]
        up = jnp.where(sub == 0, 0.0, pltpu.roll(c, 1, axis=0))
        dn = jnp.where(sub == span - 1, 0.0, pltpu.roll(c, span - 1, axis=0))
        near = (up + dn) + lane_sum(c) + (src[layer - 1] + src[layer + 1])
        return b[layer] + r[layer] * near

    source = b
    for step in range(1, SWEEPS):
        target = odd if step % 2 else even
        if step < SWEEPS - 1:

            for layer in range(step, total - step):
                target[layer] = sweep(source, layer)
        else:
            for layer in range(HALO, HALO + layers):
                value = jnp.exp(sweep(source, layer))
                out[layer - HALO] = value[ROWPAD : ROWPAD + own_rows]

        source = target


def body(axes, fine_noise, fine_kappa, coarse_kappa):
    noise = fine_noise[0, 0]
    kappa = fine_kappa[0, 0]
    depth, rows, cols = noise.shape
    layers, own_rows, half_cols = coarse_kappa.shape
    groups, slabs = lax.axis_size("grp"), lax.axis_size("slab")
    count = groups * slabs
    size = {"grp": groups, "slab": slabs}

    def flat(link):
        where = {"grp": link % groups, "slab": link // groups}
        index = 0
        for axis in axes:
            index = index * size[axis] + where[axis]
        return index

    near, far = [], []
    for link in range(count - 1):
        both = [(flat(link), flat(link + 1)), (flat(link + 1), flat(link))]
        (far if link % 2 else near).extend(both)
    position = lax.axis_index("grp")
    flip = (position % 2).astype(jnp.int32)
    flip1 = flip[None]
    place = position.astype(jnp.int32)[None]
    params = pltpu.CompilerParams(vmem_limit_bytes=LIMIT)
    cells = rows * cols
    plane = jax.ShapeDtypeStruct((rows, cols), jnp.float32)
    stack = jax.ShapeDtypeStruct((depth, rows, cols), jnp.float32)
    inner = jax.ShapeDtypeStruct((depth - 2, rows, cols), jnp.float32)

    piece_rows = rows // PIECES

    def send_far(piece):
        return lax.ppermute(piece, axes, far)

    def send_near(layer):
        return lax.ppermute(layer, axes, near)

    def face(layer):
        n = lax.dynamic_index_in_dim(noise, layer, 0, keepdims=False)
        k = lax.dynamic_index_in_dim(kappa, layer, 0, keepdims=False)
        return n / (6.0 + k)

    index_off = flip * (depth - 1)
    index_on = (1 - flip) * (depth - 1)
    off, restrict_place = lax.optimization_barrier((face(index_off), place))
    halo_off = [send_far(off[k * piece_rows : (k + 1) * piece_rows]) for k in range(PIECES)]
    halo_on = send_near(face(index_on))

    span = own_rows + 2 * ROWPAD
    part = (depth // 2) * span
    edge = layers * ROWPAD
    flats = [jax.ShapeDtypeStruct((n, half_cols), jnp.float32) for n in (2 * part + edge, part + edge, part)]
    far_send, near_send, kept = pl.pallas_call(
        restrict_kernel,
        name="restrict",
        out_shape=tuple(flats),
        in_specs=[scalar(), whole(), whole()],
        out_specs=(whole(),) * 3,
        scratch_shapes=[
            pltpu.VMEM((rows, cols), jnp.float32),
            pltpu.VMEM((rows, 128), jnp.float32),
            pltpu.VMEM((rows // 2 + 2 * ROWPAD, half_cols), jnp.float32),
        ],
        compiler_params=params,
        cost_estimate=cost(cells * depth, 8, 1),
    )(restrict_place, noise, coarse_kappa)
    across = lax.ppermute(far_send, "grp", [(g, g ^ 2) for g in range(groups)])

    b, r, part_off, part_on, mid = pl.pallas_call(
        first_kernel,
        name="first",
        out_shape=(stack, stack, plane, plane, inner),
        in_specs=[scalar(), whole(), whole()],
        out_specs=(whole(),) * 5,
        compiler_params=params,
        cost_estimate=cost(cells * depth, 16, 5),
    )(flip1, noise, kappa)

    def meet(layer, start, part, halo):
        return pl.pallas_call(
            functools.partial(meet_kernel, layer, start),
            name="meet",
            out_shape=jax.ShapeDtypeStruct(halo.shape, jnp.float32),
            in_specs=[whole()] * 3,
            out_specs=whole(),
            compiler_params=params,
            cost_estimate=cost(halo.size, 2, 4),
        )(part, halo, r)

    def meet_off(part, halos):
        return [meet(0, k * piece_rows, part, halo) for k, halo in enumerate(halos)]

    off = meet_off(part_off, halo_off)
    on = meet(depth - 1, 0, part_on, halo_on)
    halo_off = [send_far(piece) for piece in off]
    halo_on = send_near(on)
    across, off[-1] = lax.optimization_barrier((across, off[-1]))

    relayed = pl.pallas_call(
        relay_kernel,
        name="relay",
        out_shape=jax.ShapeDtypeStruct((2 * part + 2 * edge, half_cols), jnp.float32),
        in_specs=[whole()] * 2,
        out_specs=whole(),
        compiler_params=params,
        cost_estimate=cost(part * half_cols, 1, 4),
    )(near_send, across)
    near_got = lax.ppermute(relayed, "grp", [(g, g ^ 1) for g in range(groups)])
    rim = jax.ShapeDtypeStruct((2, HALO, span, half_cols), jnp.float32)
    own, up, down = pl.pallas_call(
        frame_kernel,
        name="frame",
        out_shape=(
            jax.ShapeDtypeStruct((2, layers, span, half_cols), jnp.float32),
            rim,
            rim,
        ),
        in_specs=[scalar()] + [whole()] * 4,
        out_specs=(whole(),) * 3,
        compiler_params=params,
        cost_estimate=cost(layers * span * half_cols, 4, 5),
    )(place, kept, across, near_got, coarse_kappa)
    ahead = [(i, i + 1) for i in range(slabs - 1)]
    back = [(i + 1, i) for i in range(slabs - 1)]
    below = lax.ppermute(up, "slab", ahead)
    above = lax.ppermute(down, "slab", back)

    part_off, part_on, mid = pl.pallas_call(
        middle_kernel,
        name="middle",
        out_shape=(plane, plane, inner),
        in_specs=[whole()] * (PIECES + 4),
        out_specs=(whole(),) * 3,
        scratch_shapes=[pltpu.VMEM((rows, cols), jnp.float32)],
        compiler_params=params,
        cost_estimate=cost(cells * depth, 12, 4),
    )(*off, on, mid, b, r)

    off = meet_off(part_off, halo_off)
    on = meet(depth - 1, 0, part_on, halo_on)
    halo_off = [send_far(piece) for piece in off]
    halo_on = send_near(on)
    part_off, part_on, fine = pl.pallas_call(
        last_kernel,
        name="last",
        out_shape=(plane, plane, stack),
        in_specs=[scalar()] + [whole()] * (PIECES + 4),
        out_specs=(whole(), whole(), anywhere()),
        scratch_shapes=[
            pltpu.VMEM((depth - 2, rows, cols), jnp.float32),
            pltpu.SemaphoreType.DMA((depth - 2,)),
            pltpu.VMEM((rows, cols), jnp.float32),
        ],
        compiler_params=params,
        cost_estimate=cost(cells * depth, 14, 4, cells * 2),
    )(flip1, *off, on, mid, b, r)

    framed = (layers + 2 * HALO, span, half_cols)
    coarse = pl.pallas_call(
        coarse_kernel,
        name="coarse",
        out_shape=jax.ShapeDtypeStruct(coarse_kappa.shape, jnp.float32),
        in_specs=[whole()] * 3,
        out_specs=whole(),
        scratch_shapes=[pltpu.VMEM(framed, jnp.float32)] * 4,
        compiler_params=params,
        cost_estimate=cost(layers * own_rows * half_cols, 80, 6),
    )(own, below, above)

    def finish(fine, layer, source, start, part, halo):
        return pl.pallas_call(
            functools.partial(face_kernel, source, start),
            name="face",
            out_shape=stack,
            in_specs=[scalar(), whole(), whole(), whole(), anywhere()],
            out_specs=anywhere(),
            scratch_shapes=[
                pltpu.VMEM(halo.shape, jnp.float32),
                pltpu.SemaphoreType.DMA((FACE_TILES,)),
            ],
            input_output_aliases={4: 0},
            compiler_params=params,
            cost_estimate=cost(halo.size, 3, 4, halo.size),
        )(layer[None], part, r, halo, fine)

    fine = finish(fine, index_on, depth - 1, 0, part_on, halo_on)
    for k, halo in enumerate(halo_off):
        fine = finish(fine, index_off, 0, k * piece_rows, part_off, halo)
    return fine[None, None], coarse


def solution(mesh):
    return jax.shard_map(
        functools.partial(body, tuple(mesh.axis_names)),
        mesh=mesh,
        in_specs=(
            P("slab", "grp", None, None, None),
            P("slab", "grp", None, None, None),
            P("slab", "grp", None),
        ),
        out_specs=(P("slab", "grp", None, None, None), P("slab", "grp", None)),
        check_vma=False,
    )
```

```python
import functools

import jax
import jax.numpy as jnp
from jax import lax
from jax.experimental import pallas as pl
from jax.experimental.pallas import tpu as pltpu
from jax.sharding import PartitionSpec as P

SWEEPS = 4
HALO = SWEEPS - 1
ROWPAD = 4
STRIP = 32
FACE_TILES = 2
LAST_TILES = 4
PIECES = 2
FLOPS = {"restrict": 1000000, "first": 300000000, "meet": 1000000000, "relay": 2000000000, "frame": 1000000, "middle": 10000000000, "last": 5000000000, "coarse": 1000000, "face": 5000000000}
LIMIT = 12 * 1024 * 1024


def whole():
    return pl.BlockSpec(memory_space=pltpu.VMEM)


def scalar():
    return pl.BlockSpec(memory_space=pltpu.SMEM)


def anywhere():
    return pl.BlockSpec(memory_space=pl.ANY)


def cost(name):
    return pl.CostEstimate(flops=FLOPS[name], bytes_accessed=1000000, transcendentals=0)


def lane_sum(c):
    cols = c.shape[-1]
    left = pltpu.roll(c, 1, axis=1)
    right = pltpu.roll(c, cols - 1, axis=1)
    lane = lax.broadcasted_iota(jnp.int32, (c.shape[0], 128), 1)
    total = left + right
    first = right[:, :128] + jnp.where(lane == 0, 0.0, left[:, :128])
    last = left[:, cols - 128 :] + jnp.where(lane == 127, 0.0, right[:, cols - 128 :])
    inner = [total[:, 128 : cols - 128]] if cols > 256 else []
    return jnp.concatenate([first, *inner, last], axis=1)


def plane_sum(load, start, size, rows):
    c = load(start, size)
    above = load(pl.multiple_of(jnp.maximum(start - 8, 0), 8), 8)[7:8]
    below = load(pl.multiple_of(jnp.minimum(start + size, rows - 8), 8), 8)[0:1]
    above = jnp.where(start > 0, above, 0.0)
    below = jnp.where(start + size < rows, below, 0.0)
    sub = lax.broadcasted_iota(jnp.int32, (8, c.shape[1]), 0)
    up = pltpu.roll(c, 1, axis=0)
    down = pltpu.roll(c, size - 1, axis=0)
    up = jnp.concatenate([jnp.where(sub == 0, above, up[:8]), up[8:]], axis=0)
    down = jnp.concatenate([down[: size - 8], jnp.where(sub == 7, below, down[size - 8 :])], axis=0)
    return (up + down) + lane_sum(c)


def loader(ref, *lead):
    return lambda start, size: ref[(*lead, pl.ds(start, size), slice(None))]


def strips(first, last, body):
    @pl.loop(first // STRIP, last // STRIP)
    def _(k):
        body(pl.multiple_of(k * STRIP, STRIP))


def advance(field, b, r, rows, face_off, face_on, mid, first=0, last=None):
    depth = len(field)

    def body(i):
        for m in range(depth):
            total = plane_sum(field[m], i, STRIP, rows)
            if m > 0:
                total = total + field[m - 1](i, STRIP)
            if m < depth - 1:
                total = total + field[m + 1](i, STRIP)
            rows_of = pl.ds(i, STRIP)
            value = b[m, rows_of, :] + r[m, rows_of, :] * total
            if m == 0:
                face_off[rows_of, :] = value
            elif m == depth - 1:
                face_on[rows_of, :] = value
            else:
                mid(m - 1, rows_of, value)

    strips(first, rows if last is None else last, body)


def first_kernel(flip_ref, noise, kappa, b, r, part_off, part_on, mid):
    depth, rows, _ = b.shape
    flip = flip_ref[0]

    def prepare(i):
        for m in range(depth):
            src = m + flip * (depth - 1 - 2 * m)
            at = pl.ds(i, STRIP)
            inverse = 1.0 / (6.0 + kappa[src, at, :])
            r[m, at, :] = inverse
            b[m, at, :] = noise[src, at, :] * inverse

    strips(0, rows, prepare)
    field = [loader(b, m) for m in range(depth)]

    def put(m, at, value):
        mid[m, at, :] = value

    advance(field, b, r, rows, part_off, part_on, put)


def meet_kernel(layer, start, part, halo, r, out):
    rows = out.shape[0]
    size = min(2 * STRIP, rows)
    for k in range(rows // size):
        at = pl.ds(k * size, size)
        of = pl.ds(start + k * size, size)
        out[at, :] = part[of, :] + r[layer, of, :] * halo[at, :]


def joined(pieces, whole_ref):
    rows = pieces[0].shape[0]
    for k, piece in enumerate(pieces):
        whole_ref[k * rows : (k + 1) * rows, :] = piece[...]


def middle_kernel(*refs):
    pieces = refs[:PIECES]
    on, old_mid, b, r, part_off, part_on, mid, off = refs[PIECES:]
    depth, rows, _ = b.shape
    joined(pieces, off)
    field = [loader(off)] + [loader(old_mid, m) for m in range(depth - 2)] + [loader(on)]

    def put(m, at, value):
        mid[m, at, :] = value

    advance(field, b, r, rows, part_off, part_on, put)


def last_kernel(flip_ref, *refs):
    pieces = refs[:PIECES]
    on, old_mid, b, r, part_off, part_on, out, mid, sems, off = refs[PIECES:]
    depth, rows, _ = b.shape
    joined(pieces, off)
    flip = flip_ref[0]
    field = [loader(off)] + [loader(old_mid, m) for m in range(depth - 2)] + [loader(on)]

    def put(m, at, value):
        mid[m, at, :] = jnp.exp(value)

    copies = []
    tile = rows // LAST_TILES
    for k in range(LAST_TILES):
        at = pl.ds(k * tile, tile)
        advance(field, b, r, rows, part_off, part_on, put, k * tile, (k + 1) * tile)
        for m in range(1, depth - 1):
            dst = m + flip * (depth - 1 - 2 * m)
            copies.append(
                pltpu.make_async_copy(mid.at[m - 1, at], out.at[dst, at], sems.at[m - 1, k])
            )
            copies[-1].start()
    for copy in copies:
        copy.wait()


def face_kernel(source, start, layer_ref, part, r, halo, old, out, done, sems):
    del old
    tile = halo.shape[0] // FACE_TILES
    copies = []
    for k in range(FACE_TILES):
        at = pl.ds(k * tile, tile)
        of = pl.ds(start + k * tile, tile)
        done[at, :] = jnp.exp(part[of, :] + r[source, of, :] * halo[at, :])
        copies.append(
            pltpu.make_async_copy(done.at[at], out.at[layer_ref[0], of], sems.at[k])
        )
        copies[-1].start()
    for copy in copies:
        copy.wait()


def restrict_kernel(place_ref, noise, kappa, far, near, own, pair, fine_rows, padded):
    depth, rows, cols = noise.shape
    half_rows, half_cols = rows // 2, cols // 2
    own_rows = kappa.shape[1]
    span = own_rows + 2 * ROWPAD
    part = (depth // 2) * span
    position = place_ref[0]
    src = lax.broadcasted_iota(jnp.int32, (cols, half_cols), 0)
    dst = lax.broadcasted_iota(jnp.int32, (cols, half_cols), 1)
    fold = jnp.where(src // 2 == dst, 0.125, 0.0).astype(jnp.bfloat16)
    padded[...] = jnp.zeros_like(padded)
    flip1 = 1 - 2 * (position % 2)
    other = position + flip1
    across = jnp.where(position < 2, position + 2, position - 2)
    beyond = across + flip1
    for layer in range(depth // 2):
        pair[...] = noise[2 * layer] + noise[2 * layer + 1]
        pieces = []
        for c in range(cols // 128):
            fine_rows[...] = pair[:, 128 * c : 128 * (c + 1)]
            pieces.append(
                fine_rows[pl.ds(0, half_rows, stride=2), :]
                + fine_rows[pl.ds(1, half_rows, stride=2), :]
            )
        summed = jnp.concatenate(pieces, axis=1)
        high = summed.astype(jnp.bfloat16)
        rest = summed - high.astype(jnp.float32)
        middle = rest.astype(jnp.bfloat16)
        low = (rest - middle.astype(jnp.float32)).astype(jnp.bfloat16)
        dot = functools.partial(jnp.dot, preferred_element_type=jnp.float32)
        coarse = dot(low, fold) + dot(middle, fold) + dot(high, fold)
        padded[ROWPAD : ROWPAD + half_rows, :] = coarse
        at = slice(layer * span, (layer + 1) * span)

        def rows_of(g):
            return padded[pl.ds(pl.multiple_of(g * own_rows, 8), span), :]

        own[at, :] = rows_of(position)
        near[at, :] = rows_of(other)
        far[at, :] = rows_of(across)
        far[part + layer * span : part + (layer + 1) * span, :] = rows_of(beyond)
    for layer in range(kappa.shape[0]):
        first = 1.0 / (1.5 + kappa[layer, 0:ROWPAD, :])
        last = 1.0 / (1.5 + kappa[layer, own_rows - ROWPAD : own_rows, :])
        at = layer * ROWPAD
        far[2 * part + at : 2 * part + at + ROWPAD, :] = jnp.where(position < 2, last, first)
        near[part + at : part + at + ROWPAD, :] = jnp.where(position % 2 == 0, last, first)


def relay_kernel(near, arrived, out):
    mine = near.shape[0]
    carried = out.shape[0] - mine
    out[0:mine, :] = near[...]
    out[mine:, :] = arrived[arrived.shape[0] - carried :, :]


def frame_kernel(place_ref, kept, across, near, kappa, own, up, down):
    layers, own_rows, _ = kappa.shape
    span = own_rows + 2 * ROWPAD
    per = kept.shape[0] // span
    part = per * span
    edge = layers * ROWPAD
    position = place_ref[0]
    flip1 = 1 - 2 * (position % 2)
    beyond_chip = jnp.where(position < 2, position + 2, position - 2)
    for k in range(per):
        at = slice(k * span, (k + 1) * span)
        own[0, per * position + k] = kept[at, :]
        own[0, per * (position + flip1) + k] = near[at, :]
        own[0, per * beyond_chip + k] = across[at, :]
        relayed = slice(part + edge + k * span, part + edge + (k + 1) * span)
        own[0, per * (beyond_chip + flip1) + k] = near[relayed, :]
    for layer in range(layers):
        at = layer * ROWPAD
        direct = near[part + at : part + at + ROWPAD, :]
        passed = near[2 * part + edge + at : 2 * part + edge + at + ROWPAD, :]
        inner = jnp.logical_or(position == 1, position == 2)
        passed = jnp.where(inner, passed, 0.0)
        even = position % 2 == 0
        top = jnp.where(even, passed, direct)
        bottom = jnp.where(even, direct, passed)
        middle = 1.0 / (1.5 + kappa[layer])
        own[1, layer] = jnp.concatenate([top, middle, bottom], axis=0)
    for out, layer_at in ((down, lambda d: d - 1), (up, lambda d: layers - d)):
        base = 0
        for distance in range(1, HALO + 1):
            layer = layer_at(distance)
            trim = ROWPAD - HALO + distance
            at = slice(trim, span - trim)
            noise, inverse = own[0, layer, at, :], own[1, layer, at, :]
            values = (noise, inverse) if distance < HALO else (noise * inverse,)
            for value in values:
                out[base : base + span - 2 * trim, :] = value
                base += span - 2 * trim


def rim_rows(span):
    kept = [span - 2 * (ROWPAD - HALO + distance) for distance in range(1, HALO + 1)]
    return 2 * sum(kept[:-1]) + kept[-1]


def coarse_kernel(own, below, above, out, b, r, even, odd):
    layers, own_rows, _ = out.shape
    total_layers, span, cols = b.shape
    total = total_layers

    def prepare(dst, ref, src):
        inverse = ref[1, src]
        r[dst] = 0.25 * inverse
        b[dst] = ref[0, src] * inverse

    for ref, layer_at in (
        (below, lambda d: HALO - d),
        (above, lambda d: HALO + layers - 1 + d),
    ):
        base = 0
        for distance in range(1, HALO + 1):
            layer = layer_at(distance)
            trim = ROWPAD - HALO + distance
            size = span - 2 * trim
            at = slice(trim, span - trim)
            b[layer] = jnp.zeros((span, cols), jnp.float32)
            r[layer] = jnp.zeros((span, cols), jnp.float32)
            value = ref[base : base + size, :]
            base += size
            if distance < HALO:
                inverse = ref[base : base + size, :]
                base += size
                value = value * inverse
                r[layer, at, :] = 0.25 * inverse
            b[layer, at, :] = value

    for k in range(layers):
        prepare(HALO + k, own, k)

    sub = lax.broadcasted_iota(jnp.int32, (span, cols), 0)

    def sweep(src, layer):
        c = src[layer]
        up = jnp.where(sub == 0, 0.0, pltpu.roll(c, 1, axis=0))
        dn = jnp.where(sub == span - 1, 0.0, pltpu.roll(c, span - 1, axis=0))
        near = (up + dn) + lane_sum(c) + (src[layer - 1] + src[layer + 1])
        return b[layer] + r[layer] * near

    source = b
    for step in range(1, SWEEPS):
        target = odd if step % 2 else even
        if step < SWEEPS - 1:

            for layer in range(step, total - step):
                target[layer] = sweep(source, layer)
        else:
            for layer in range(HALO, HALO + layers):
                value = jnp.exp(sweep(source, layer))
                out[layer - HALO] = value[ROWPAD : ROWPAD + own_rows]

        source = target


def body(axes, fine_noise, fine_kappa, coarse_kappa):
    noise = fine_noise[0, 0]
    kappa = fine_kappa[0, 0]
    depth, rows, cols = noise.shape
    layers, own_rows, half_cols = coarse_kappa.shape
    groups, slabs = lax.axis_size("grp"), lax.axis_size("slab")
    count = groups * slabs
    size = {"grp": groups, "slab": slabs}

    def flat(link):
        where = {"grp": link % groups, "slab": link // groups}
        index = 0
        for axis in axes:
            index = index * size[axis] + where[axis]
        return index

    near, far = [], []
    for link in range(count - 1):
        both = [(flat(link), flat(link + 1)), (flat(link + 1), flat(link))]
        (far if link % 2 else near).extend(both)
    position = lax.axis_index("grp")
    flip = (position % 2).astype(jnp.int32)
    flip1 = flip[None]
    place = position.astype(jnp.int32)[None]
    params = pltpu.CompilerParams(vmem_limit_bytes=LIMIT)
    cells = rows * cols
    plane = jax.ShapeDtypeStruct((rows, cols), jnp.float32)
    stack = jax.ShapeDtypeStruct((depth, rows, cols), jnp.float32)
    inner = jax.ShapeDtypeStruct((depth - 2, rows, cols), jnp.float32)

    piece_rows = rows // PIECES

    def send_far(piece):
        return lax.ppermute(piece, axes, far)

    def send_near(layer):
        return lax.ppermute(layer, axes, near)

    def face(layer):
        n = lax.dynamic_index_in_dim(noise, layer, 0, keepdims=False)
        k = lax.dynamic_index_in_dim(kappa, layer, 0, keepdims=False)
        return n / (6.0 + k)

    index_off = flip * (depth - 1)
    index_on = (1 - flip) * (depth - 1)
    off, restrict_place = lax.optimization_barrier((face(index_off), place))
    halo_off = [send_far(off[k * piece_rows : (k + 1) * piece_rows]) for k in range(PIECES)]
    halo_on = send_near(face(index_on))

    span = own_rows + 2 * ROWPAD
    part = (depth // 2) * span
    edge = layers * ROWPAD
    flats = [jax.ShapeDtypeStruct((n, half_cols), jnp.float32) for n in (2 * part + edge, part + edge, part)]
    far_send, near_send, kept = pl.pallas_call(
        restrict_kernel,
        name="restrict",
        out_shape=tuple(flats),
        in_specs=[scalar(), whole(), whole()],
        out_specs=(whole(),) * 3,
        scratch_shapes=[
            pltpu.VMEM((rows, cols), jnp.float32),
            pltpu.VMEM((rows, 128), jnp.float32),
            pltpu.VMEM((rows // 2 + 2 * ROWPAD, half_cols), jnp.float32),
        ],
        compiler_params=params,
        cost_estimate=cost("restrict"),
    )(restrict_place, noise, coarse_kappa)
    across = lax.ppermute(far_send, "grp", [(g, g ^ 2) for g in range(groups)])

    b, r, part_off, part_on, mid = pl.pallas_call(
        first_kernel,
        name="first",
        out_shape=(stack, stack, plane, plane, inner),
        in_specs=[scalar(), whole(), whole()],
        out_specs=(whole(),) * 5,
        compiler_params=params,
        cost_estimate=cost("first"),
    )(flip1, noise, kappa)

    def meet(layer, start, part, halo):
        return pl.pallas_call(
            functools.partial(meet_kernel, layer, start),
            name="meet",
            out_shape=jax.ShapeDtypeStruct(halo.shape, jnp.float32),
            in_specs=[whole()] * 3,
            out_specs=whole(),
            compiler_params=params,
            cost_estimate=cost("meet"),
        )(part, halo, r)

    def meet_off(part, halos):
        return [meet(0, k * piece_rows, part, halo) for k, halo in enumerate(halos)]

    off = meet_off(part_off, halo_off)
    on = meet(depth - 1, 0, part_on, halo_on)
    halo_off = [send_far(piece) for piece in off]
    halo_on = send_near(on)
    across, off[-1] = lax.optimization_barrier((across, off[-1]))

    relayed = pl.pallas_call(
        relay_kernel,
        name="relay",
        out_shape=jax.ShapeDtypeStruct((2 * part + 2 * edge, half_cols), jnp.float32),
        in_specs=[whole()] * 2,
        out_specs=whole(),
        compiler_params=params,
        cost_estimate=cost("relay"),
    )(near_send, across)
    near_got = lax.ppermute(relayed, "grp", [(g, g ^ 1) for g in range(groups)])
    rim = jax.ShapeDtypeStruct((rim_rows(span), half_cols), jnp.float32)
    own, up, down = pl.pallas_call(
        frame_kernel,
        name="frame",
        out_shape=(
            jax.ShapeDtypeStruct((2, layers, span, half_cols), jnp.float32),
            rim,
            rim,
        ),
        in_specs=[scalar()] + [whole()] * 4,
        out_specs=(whole(),) * 3,
        compiler_params=params,
        cost_estimate=cost("frame"),
    )(place, kept, across, near_got, coarse_kappa)
    ahead = [(i, i + 1) for i in range(slabs - 1)]
    back = [(i + 1, i) for i in range(slabs - 1)]
    below = lax.ppermute(up, "slab", ahead)
    above = lax.ppermute(down, "slab", back)

    part_off, part_on, mid = pl.pallas_call(
        middle_kernel,
        name="middle",
        out_shape=(plane, plane, inner),
        in_specs=[whole()] * (PIECES + 4),
        out_specs=(whole(),) * 3,
        scratch_shapes=[pltpu.VMEM((rows, cols), jnp.float32)],
        compiler_params=params,
        cost_estimate=cost("middle"),
    )(*off, on, mid, b, r)

    off = meet_off(part_off, halo_off)
    on = meet(depth - 1, 0, part_on, halo_on)
    halo_off = [send_far(piece) for piece in off]
    halo_on = send_near(on)
    part_off, part_on, fine = pl.pallas_call(
        last_kernel,
        name="last",
        out_shape=(plane, plane, stack),
        in_specs=[scalar()] + [whole()] * (PIECES + 4),
        out_specs=(whole(), whole(), anywhere()),
        scratch_shapes=[
            pltpu.VMEM((depth - 2, rows, cols), jnp.float32),
            pltpu.SemaphoreType.DMA((depth - 2, LAST_TILES)),
            pltpu.VMEM((rows, cols), jnp.float32),
        ],
        compiler_params=params,
        cost_estimate=cost("last"),
    )(flip1, *off, on, mid, b, r)

    framed = (layers + 2 * HALO, span, half_cols)
    coarse = pl.pallas_call(
        coarse_kernel,
        name="coarse",
        out_shape=jax.ShapeDtypeStruct(coarse_kappa.shape, jnp.float32),
        in_specs=[whole()] * 3,
        out_specs=whole(),
        scratch_shapes=[pltpu.VMEM(framed, jnp.float32)] * 4,
        compiler_params=params,
        cost_estimate=cost("coarse"),
    )(own, below, above)

    def finish(fine, layer, source, start, part, halo):
        return pl.pallas_call(
            functools.partial(face_kernel, source, start),
            name="face",
            out_shape=stack,
            in_specs=[scalar(), whole(), whole(), whole(), anywhere()],
            out_specs=anywhere(),
            scratch_shapes=[
                pltpu.VMEM(halo.shape, jnp.float32),
                pltpu.SemaphoreType.DMA((FACE_TILES,)),
            ],
            input_output_aliases={4: 0},
            compiler_params=params,
            cost_estimate=cost("face"),
        )(layer[None], part, r, halo, fine)

    fine = finish(fine, index_on, depth - 1, 0, part_on, halo_on)
    for k, halo in enumerate(halo_off):
        fine = finish(fine, index_off, 0, k * piece_rows, part_off, halo)
    return fine[None, None], coarse


def solution(mesh):
    return jax.shard_map(
        functools.partial(body, tuple(mesh.axis_names)),
        mesh=mesh,
        in_specs=(
            P("slab", "grp", None, None, None),
            P("slab", "grp", None, None, None),
            P("slab", "grp", None),
        ),
        out_specs=(P("slab", "grp", None, None, None), P("slab", "grp", None)),
        check_vma=False,
    )
```

```python
import functools

import jax
import jax.numpy as jnp
from jax import lax
from jax.experimental import pallas as pl
from jax.experimental.pallas import tpu as pltpu
from jax.sharding import PartitionSpec as P

SWEEPS = 4
HALO = SWEEPS - 1
ROWPAD = 4
STRIP = 32
FACE_TILES = 2
LAST_TILES = 4
PIECES = 2
FLOPS = {"restrict": 1000000, "first": 300000000, "meet": 1000000000, "relay": 2000000000, "frame": 1000000, "middle": 10000000000, "last": 5000000000, "coarse": 1000000, "face": 5000000000}
LIMIT = 12 * 1024 * 1024


def whole():
    return pl.BlockSpec(memory_space=pltpu.VMEM)


def scalar():
    return pl.BlockSpec(memory_space=pltpu.SMEM)


def anywhere():
    return pl.BlockSpec(memory_space=pl.ANY)


def cost(name):
    return pl.CostEstimate(flops=FLOPS[name], bytes_accessed=1000000, transcendentals=0)


def lane_sum(c):
    cols = c.shape[-1]
    left = pltpu.roll(c, 1, axis=1)
    right = pltpu.roll(c, cols - 1, axis=1)
    lane = lax.broadcasted_iota(jnp.int32, (c.shape[0], 128), 1)
    total = left + right
    first = right[:, :128] + jnp.where(lane == 0, 0.0, left[:, :128])
    last = left[:, cols - 128 :] + jnp.where(lane == 127, 0.0, right[:, cols - 128 :])
    inner = [total[:, 128 : cols - 128]] if cols > 256 else []
    return jnp.concatenate([first, *inner, last], axis=1)


def plane_sum(load, start, size, rows):
    c = load(start, size)
    above = load(pl.multiple_of(jnp.maximum(start - 8, 0), 8), 8)[7:8]
    below = load(pl.multiple_of(jnp.minimum(start + size, rows - 8), 8), 8)[0:1]
    above = jnp.where(start > 0, above, 0.0)
    below = jnp.where(start + size < rows, below, 0.0)
    sub = lax.broadcasted_iota(jnp.int32, (8, c.shape[1]), 0)
    up = pltpu.roll(c, 1, axis=0)
    down = pltpu.roll(c, size - 1, axis=0)
    up = jnp.concatenate([jnp.where(sub == 0, above, up[:8]), up[8:]], axis=0)
    down = jnp.concatenate([down[: size - 8], jnp.where(sub == 7, below, down[size - 8 :])], axis=0)
    return (up + down) + lane_sum(c)


def loader(ref, *lead):
    return lambda start, size: ref[(*lead, pl.ds(start, size), slice(None))]


def strips(first, last, body):
    @pl.loop(first // STRIP, last // STRIP)
    def _(k):
        body(pl.multiple_of(k * STRIP, STRIP))


def advance(field, b, r, rows, face_off, face_on, mid, first=0, last=None):
    depth = len(field)

    def body(i):
        for m in range(depth):
            total = plane_sum(field[m], i, STRIP, rows)
            if m > 0:
                total = total + field[m - 1](i, STRIP)
            if m < depth - 1:
                total = total + field[m + 1](i, STRIP)
            rows_of = pl.ds(i, STRIP)
            value = b[m, rows_of, :] + r[m, rows_of, :] * total
            if m == 0:
                face_off[rows_of, :] = value
            elif m == depth - 1:
                face_on[rows_of, :] = value
            else:
                mid(m - 1, rows_of, value)

    strips(first, rows if last is None else last, body)


def first_kernel(flip_ref, noise, kappa, b, r, part_off, part_on, mid):
    depth, rows, _ = b.shape
    flip = flip_ref[0]

    def prepare(i):
        for m in range(depth):
            src = m + flip * (depth - 1 - 2 * m)
            at = pl.ds(i, STRIP)
            inverse = 1.0 / (6.0 + kappa[src, at, :])
            r[m, at, :] = inverse
            b[m, at, :] = noise[src, at, :] * inverse

    strips(0, rows, prepare)
    field = [loader(b, m) for m in range(depth)]

    def put(m, at, value):
        mid[m, at, :] = value

    advance(field, b, r, rows, part_off, part_on, put)


def meet_kernel(layer, start, part, halo, r, out):
    rows = out.shape[0]
    size = min(2 * STRIP, rows)
    for k in range(rows // size):
        at = pl.ds(k * size, size)
        of = pl.ds(start + k * size, size)
        out[at, :] = part[of, :] + r[layer, of, :] * halo[at, :]


def joined(pieces, whole_ref):
    rows = pieces[0].shape[0]
    for k, piece in enumerate(pieces):
        whole_ref[k * rows : (k + 1) * rows, :] = piece[...]


def middle_kernel(*refs):
    pieces = refs[:PIECES]
    on, old_mid, b, r, part_off, part_on, mid, off = refs[PIECES:]
    depth, rows, _ = b.shape
    joined(pieces, off)
    field = [loader(off)] + [loader(old_mid, m) for m in range(depth - 2)] + [loader(on)]

    def put(m, at, value):
        mid[m, at, :] = value

    advance(field, b, r, rows, part_off, part_on, put)


def last_kernel(flip_ref, *refs):
    pieces = refs[:PIECES]
    on, old_mid, b, r, part_off, part_on, out, mid, sems, off = refs[PIECES:]
    depth, rows, _ = b.shape
    joined(pieces, off)
    flip = flip_ref[0]
    field = [loader(off)] + [loader(old_mid, m) for m in range(depth - 2)] + [loader(on)]

    def put(m, at, value):
        mid[m, at, :] = jnp.exp(value)

    copies = []
    tile = rows // LAST_TILES
    for k in range(LAST_TILES):
        at = pl.ds(k * tile, tile)
        advance(field, b, r, rows, part_off, part_on, put, k * tile, (k + 1) * tile)
        for m in range(1, depth - 1):
            dst = m + flip * (depth - 1 - 2 * m)
            copies.append(
                pltpu.make_async_copy(mid.at[m - 1, at], out.at[dst, at], sems.at[m - 1, k])
            )
            copies[-1].start()
    for copy in copies:
        copy.wait()


def face_kernel(source, start, layer_ref, part, r, halo, old, out, done, sems):
    del old
    tile = halo.shape[0] // FACE_TILES
    copies = []
    for k in range(FACE_TILES):
        at = pl.ds(k * tile, tile)
        of = pl.ds(start + k * tile, tile)
        done[at, :] = jnp.exp(part[of, :] + r[source, of, :] * halo[at, :])
        copies.append(
            pltpu.make_async_copy(done.at[at], out.at[layer_ref[0], of], sems.at[k])
        )
        copies[-1].start()
    for copy in copies:
        copy.wait()


def restrict_kernel(place_ref, noise, kappa, far, near, own, pair, fine_rows, padded):
    depth, rows, cols = noise.shape
    half_rows, half_cols = rows // 2, cols // 2
    own_rows = kappa.shape[1]
    span = own_rows + 2 * ROWPAD
    part = (depth // 2) * span
    position = place_ref[0]
    src = lax.broadcasted_iota(jnp.int32, (cols, half_cols), 0)
    dst = lax.broadcasted_iota(jnp.int32, (cols, half_cols), 1)
    fold = jnp.where(src // 2 == dst, 0.125, 0.0).astype(jnp.bfloat16)
    padded[...] = jnp.zeros_like(padded)
    flip1 = 1 - 2 * (position % 2)
    other = position + flip1
    across = 3 - position
    beyond = across - flip1
    for layer in range(depth // 2):
        pair[...] = noise[2 * layer] + noise[2 * layer + 1]
        pieces = []
        for c in range(cols // 128):
            fine_rows[...] = pair[:, 128 * c : 128 * (c + 1)]
            pieces.append(
                fine_rows[pl.ds(0, half_rows, stride=2), :]
                + fine_rows[pl.ds(1, half_rows, stride=2), :]
            )
        summed = jnp.concatenate(pieces, axis=1)
        high = summed.astype(jnp.bfloat16)
        rest = summed - high.astype(jnp.float32)
        middle = rest.astype(jnp.bfloat16)
        low = (rest - middle.astype(jnp.float32)).astype(jnp.bfloat16)
        dot = functools.partial(jnp.dot, preferred_element_type=jnp.float32)
        coarse = dot(low, fold) + dot(middle, fold) + dot(high, fold)
        padded[ROWPAD : ROWPAD + half_rows, :] = coarse
        at = slice(layer * span, (layer + 1) * span)

        def rows_of(g):
            return padded[pl.ds(pl.multiple_of(g * own_rows, 8), span), :]

        own[at, :] = rows_of(position)
        near[at, :] = rows_of(other)
        far[at, :] = rows_of(across)
        far[part + layer * span : part + (layer + 1) * span, :] = rows_of(beyond)
    for layer in range(kappa.shape[0]):
        first = 1.0 / (1.5 + kappa[layer, 0:ROWPAD, :])
        last = 1.0 / (1.5 + kappa[layer, own_rows - ROWPAD : own_rows, :])
        at = layer * ROWPAD
        far[2 * part + at : 2 * part + at + ROWPAD, :] = jnp.where(position < 2, last, first)
        near[part + at : part + at + ROWPAD, :] = jnp.where(position % 2 == 0, last, first)


def relay_kernel(near, arrived, out):
    mine = near.shape[0]
    carried = out.shape[0] - mine
    out[0:mine, :] = near[...]
    out[mine:, :] = arrived[carried : 2 * carried, :]


def frame_kernel(place_ref, slab_ref, kept, across, near, kappa, own, even_out, odd_out):
    layers, own_rows, _ = kappa.shape
    span = own_rows + 2 * ROWPAD
    per = kept.shape[0] // span
    part = per * span
    edge = layers * ROWPAD
    position = place_ref[0]
    flip1 = 1 - 2 * (position % 2)
    beyond_chip = 3 - position
    for k in range(per):
        at = slice(k * span, (k + 1) * span)
        own[0, per * position + k] = kept[at, :]
        own[0, per * (position + flip1) + k] = near[at, :]
        own[0, per * beyond_chip + k] = across[at, :]
        relayed = slice(part + edge + k * span, part + edge + (k + 1) * span)
        own[0, per * (beyond_chip - flip1) + k] = near[relayed, :]
    for layer in range(layers):
        at = layer * ROWPAD
        direct = near[part + at : part + at + ROWPAD, :]
        passed = across[2 * part + at : 2 * part + at + ROWPAD, :]
        inner = jnp.logical_or(position == 1, position == 2)
        passed = jnp.where(inner, passed, 0.0)
        even = position % 2 == 0
        top = jnp.where(even, passed, direct)
        bottom = jnp.where(even, direct, passed)
        middle = 1.0 / (1.5 + kappa[layer])
        own[1, layer] = jnp.concatenate([top, middle, bottom], axis=0)
    even_slab = slab_ref[0] % 2 == 0
    base = 0
    for distance in range(1, HALO + 1):
        trim = ROWPAD - HALO + distance
        at = slice(trim, span - trim)
        pairs = []
        for layer in (layers - distance, distance - 1):
            noise, inverse = own[0, layer, at, :], own[1, layer, at, :]
            pairs.append((noise, inverse) if distance < HALO else (noise * inverse,))
        for up, down in zip(*pairs):
            to = slice(base, base + span - 2 * trim)
            even_out[to, :] = jnp.where(even_slab, up, down)
            odd_out[to, :] = jnp.where(even_slab, down, up)
            base += span - 2 * trim


def rim_rows(span):
    kept = [span - 2 * (ROWPAD - HALO + distance) for distance in range(1, HALO + 1)]
    return 2 * sum(kept[:-1]) + kept[-1]


def coarse_kernel(slab_ref, own, even_in, odd_in, out, b, r, even, odd):
    even_slab = slab_ref[0] % 2 == 0
    layers, own_rows, _ = out.shape
    total_layers, span, cols = b.shape
    total = total_layers

    def prepare(dst, ref, src):
        inverse = ref[1, src]
        r[dst] = 0.25 * inverse
        b[dst] = ref[0, src] * inverse

    for lower, layer_at in (
        (True, lambda d: HALO - d),
        (False, lambda d: HALO + layers - 1 + d),
    ):
        first, second = (odd_in, even_in) if lower else (even_in, odd_in)

        base = 0
        for distance in range(1, HALO + 1):
            layer = layer_at(distance)
            trim = ROWPAD - HALO + distance
            size = span - 2 * trim
            at = slice(trim, span - trim)
            b[layer] = jnp.zeros((span, cols), jnp.float32)
            r[layer] = jnp.zeros((span, cols), jnp.float32)
            at_rows = slice(base, base + size)
            value = jnp.where(even_slab, first[at_rows, :], second[at_rows, :])
            base += size
            if distance < HALO:
                at_rows = slice(base, base + size)
                inverse = jnp.where(even_slab, first[at_rows, :], second[at_rows, :])
                base += size
                value = value * inverse
                r[layer, at, :] = 0.25 * inverse
            b[layer, at, :] = value

    for k in range(layers):
        prepare(HALO + k, own, k)

    sub = lax.broadcasted_iota(jnp.int32, (span, cols), 0)

    def sweep(src, layer):
        c = src[layer]
        up = jnp.where(sub == 0, 0.0, pltpu.roll(c, 1, axis=0))
        dn = jnp.where(sub == span - 1, 0.0, pltpu.roll(c, span - 1, axis=0))
        near = (up + dn) + lane_sum(c) + (src[layer - 1] + src[layer + 1])
        return b[layer] + r[layer] * near

    source = b
    for step in range(1, SWEEPS):
        target = odd if step % 2 else even
        if step < SWEEPS - 1:

            for layer in range(step, total - step):
                target[layer] = sweep(source, layer)
        else:
            for layer in range(HALO, HALO + layers):
                value = jnp.exp(sweep(source, layer))
                out[layer - HALO] = value[ROWPAD : ROWPAD + own_rows]

        source = target


def body(axes, fine_noise, fine_kappa, coarse_kappa):
    noise = fine_noise[0, 0]
    kappa = fine_kappa[0, 0]
    depth, rows, cols = noise.shape
    layers, own_rows, half_cols = coarse_kappa.shape
    groups, slabs = lax.axis_size("grp"), lax.axis_size("slab")
    count = groups * slabs
    size = {"grp": groups, "slab": slabs}

    def flat(link):
        where = {"grp": link % groups, "slab": link // groups}
        index = 0
        for axis in axes:
            index = index * size[axis] + where[axis]
        return index

    near, far = [], []
    for link in range(count - 1):
        both = [(flat(link), flat(link + 1)), (flat(link + 1), flat(link))]
        (far if link % 2 else near).extend(both)
    position = lax.axis_index("grp")
    flip = (position % 2).astype(jnp.int32)
    flip1 = flip[None]
    place = position.astype(jnp.int32)[None]
    slab_place = lax.axis_index("slab").astype(jnp.int32)[None]
    params = pltpu.CompilerParams(vmem_limit_bytes=LIMIT)
    cells = rows * cols
    plane = jax.ShapeDtypeStruct((rows, cols), jnp.float32)
    stack = jax.ShapeDtypeStruct((depth, rows, cols), jnp.float32)
    inner = jax.ShapeDtypeStruct((depth - 2, rows, cols), jnp.float32)

    piece_rows = rows // PIECES

    def send_far(piece):
        return lax.ppermute(piece, axes, far)

    def send_near(layer):
        return lax.ppermute(layer, axes, near)

    def face(layer):
        n = lax.dynamic_index_in_dim(noise, layer, 0, keepdims=False)
        k = lax.dynamic_index_in_dim(kappa, layer, 0, keepdims=False)
        return n / (6.0 + k)

    index_off = flip * (depth - 1)
    index_on = (1 - flip) * (depth - 1)
    index_off, place, slab_place = lax.optimization_barrier((index_off, place, slab_place))
    off, restrict_place = lax.optimization_barrier((face(index_off), place))
    halo_off = [send_far(off[k * piece_rows : (k + 1) * piece_rows]) for k in range(PIECES)]
    halo_on = send_near(face(index_on))

    span = own_rows + 2 * ROWPAD
    part = (depth // 2) * span
    edge = layers * ROWPAD
    flats = [jax.ShapeDtypeStruct((n, half_cols), jnp.float32) for n in (2 * part + edge, part + edge, part)]
    far_send, near_send, kept = pl.pallas_call(
        restrict_kernel,
        name="restrict",
        out_shape=tuple(flats),
        in_specs=[scalar(), whole(), whole()],
        out_specs=(whole(),) * 3,
        scratch_shapes=[
            pltpu.VMEM((rows, cols), jnp.float32),
            pltpu.VMEM((rows, 128), jnp.float32),
            pltpu.VMEM((rows // 2 + 2 * ROWPAD, half_cols), jnp.float32),
        ],
        compiler_params=params,
        cost_estimate=cost("restrict"),
    )(restrict_place, noise, coarse_kappa)
    across = lax.ppermute(far_send, "grp", [(g, g ^ 3) for g in range(groups)])

    b, r, part_off, part_on, mid = pl.pallas_call(
        first_kernel,
        name="first",
        out_shape=(stack, stack, plane, plane, inner),
        in_specs=[scalar(), whole(), whole()],
        out_specs=(whole(),) * 5,
        compiler_params=params,
        cost_estimate=cost("first"),
    )(flip1, noise, kappa)

    def meet(layer, start, part, halo):
        return pl.pallas_call(
            functools.partial(meet_kernel, layer, start),
            name="meet",
            out_shape=jax.ShapeDtypeStruct(halo.shape, jnp.float32),
            in_specs=[whole()] * 3,
            out_specs=whole(),
            compiler_params=params,
            cost_estimate=cost("meet"),
        )(part, halo, r)

    def meet_off(part, halos):
        return [meet(0, k * piece_rows, part, halo) for k, halo in enumerate(halos)]

    off = meet_off(part_off, halo_off)
    on = meet(depth - 1, 0, part_on, halo_on)
    halo_off = [send_far(piece) for piece in off]
    halo_on = send_near(on)
    across, off[0] = lax.optimization_barrier((across, off[0]))

    relayed = pl.pallas_call(
        relay_kernel,
        name="relay",
        out_shape=jax.ShapeDtypeStruct((2 * part + edge, half_cols), jnp.float32),
        in_specs=[whole()] * 2,
        out_specs=whole(),
        compiler_params=params,
        cost_estimate=cost("relay"),
    )(near_send, across)
    near_got = lax.ppermute(relayed, "grp", [(g, g ^ 1) for g in range(groups)])
    rim = jax.ShapeDtypeStruct((rim_rows(span), half_cols), jnp.float32)
    own, even_send, odd_send = pl.pallas_call(
        frame_kernel,
        name="frame",
        out_shape=(
            jax.ShapeDtypeStruct((2, layers, span, half_cols), jnp.float32),
            rim,
            rim,
        ),
        in_specs=[scalar(), scalar()] + [whole()] * 4,
        out_specs=(whole(),) * 3,
        compiler_params=params,
        cost_estimate=cost("frame"),
    )(place, slab_place, kept, across, near_got, coarse_kappa)
    even_pairs, odd_pairs = [], []
    for k in range(slabs - 1):
        (odd_pairs if k % 2 else even_pairs).extend([(k, k + 1), (k + 1, k)])
    even_got = lax.ppermute(even_send, "slab", even_pairs)
    odd_got = lax.ppermute(odd_send, "slab", odd_pairs)

    part_off, part_on, mid = pl.pallas_call(
        middle_kernel,
        name="middle",
        out_shape=(plane, plane, inner),
        in_specs=[whole()] * (PIECES + 4),
        out_specs=(whole(),) * 3,
        scratch_shapes=[pltpu.VMEM((rows, cols), jnp.float32)],
        compiler_params=params,
        cost_estimate=cost("middle"),
    )(*off, on, mid, b, r)

    off = meet_off(part_off, halo_off)
    on = meet(depth - 1, 0, part_on, halo_on)
    halo_off = [send_far(piece) for piece in off]
    halo_on = send_near(on)
    part_off, part_on, fine = pl.pallas_call(
        last_kernel,
        name="last",
        out_shape=(plane, plane, stack),
        in_specs=[scalar()] + [whole()] * (PIECES + 4),
        out_specs=(whole(), whole(), anywhere()),
        scratch_shapes=[
            pltpu.VMEM((depth - 2, rows, cols), jnp.float32),
            pltpu.SemaphoreType.DMA((depth - 2, LAST_TILES)),
            pltpu.VMEM((rows, cols), jnp.float32),
        ],
        compiler_params=params,
        cost_estimate=cost("last"),
    )(flip1, *off, on, mid, b, r)

    framed = (layers + 2 * HALO, span, half_cols)
    coarse = pl.pallas_call(
        coarse_kernel,
        name="coarse",
        out_shape=jax.ShapeDtypeStruct(coarse_kappa.shape, jnp.float32),
        in_specs=[scalar()] + [whole()] * 3,
        out_specs=whole(),
        scratch_shapes=[pltpu.VMEM(framed, jnp.float32)] * 4,
        compiler_params=params,
        cost_estimate=cost("coarse"),
    )(slab_place, own, even_got, odd_got)

    def finish(fine, layer, source, start, part, halo):
        return pl.pallas_call(
            functools.partial(face_kernel, source, start),
            name="face",
            out_shape=stack,
            in_specs=[scalar(), whole(), whole(), whole(), anywhere()],
            out_specs=anywhere(),
            scratch_shapes=[
                pltpu.VMEM(halo.shape, jnp.float32),
                pltpu.SemaphoreType.DMA((FACE_TILES,)),
            ],
            input_output_aliases={4: 0},
            compiler_params=params,
            cost_estimate=cost("face"),
        )(layer[None], part, r, halo, fine)

    fine = finish(fine, index_on, depth - 1, 0, part_on, halo_on)
    for k, halo in enumerate(halo_off):
        fine = finish(fine, index_off, 0, k * piece_rows, part_off, halo)
    return fine[None, None], coarse


def solution(mesh):
    return jax.shard_map(
        functools.partial(body, tuple(mesh.axis_names)),
        mesh=mesh,
        in_specs=(
            P("slab", "grp", None, None, None),
            P("slab", "grp", None, None, None),
            P("slab", "grp", None),
        ),
        out_specs=(P("slab", "grp", None, None, None), P("slab", "grp", None)),
        check_vma=False,
    )
```
